32 devices in a mesh: rep: 4 (over x, core), shard: 8 (over z, y).
Axes of the slice: x: 2, y: 2, z: 4, core: 2. Of those that a mesh axis runs over, the one named last changes fastest.
Arguments:
- tokens: bfloat16 [16384, 768], P(('rep', 'shard')), may hold values from -6 to 6
- segment_ids: int32 [16384], P(('rep', 'shard')), may hold values from 0 to 511, never falling along the last dimension, each value on 1 to 512 neighbouring positions
- buckets: int32 [1023], replicated, may hold values from 0 to 31
- w_query: bfloat16 [768, 768], P('shard'), may hold values from -0.21875 to 0.21875
- w_key: bfloat16 [768, 768], P('shard'), may hold values from -0.21875 to 0.21875
- w_value: bfloat16 [768, 768], P('shard'), may hold values from -0.21875 to 0.21875
- w_output: bfloat16 [768, 768], P('shard'), may hold values from -0.625 to 0.625
- w_gate: bfloat16 [768, 2048], P('shard'), may hold values from -0.21875 to 0.21875
- w_up: bfloat16 [768, 2048], P('shard'), may hold values from -0.21875 to 0.21875
- w_down: bfloat16 [2048, 768], P('shard'), may hold values from -0.125 to 0.125
- norm_attn: bfloat16 [768], P('shard'), may hold values from 0.099609375 to 1.8984375
- norm_ffn: bfloat16 [768], P('shard'), may hold values from 0.099609375 to 1.8984375
- rel_bias: bfloat16 [32, 12], P('shard'), may hold values from -4 to 4
- cotangent: bfloat16 [16384, 768], P(('rep', 'shard')), may hold values from -6 to 6
Outputs:
- output: bfloat16 [16384, 768], P(('rep', 'shard'))
- grad_tokens: bfloat16 [16384, 768], P(('rep', 'shard'))
- grad_w_query: float32 [768, 768], P('shard')
- grad_w_key: float32 [768, 768], P('shard')
- grad_w_value: float32 [768, 768], P('shard')
- grad_w_output: float32 [768, 768], P('shard')
- grad_w_gate: float32 [768, 2048], P('shard')
- grad_w_up: float32 [768, 2048], P('shard')
- grad_w_down: float32 [2048, 768], P('shard')
- grad_norm_attn: float32 [768], P('shard')
- grad_norm_ffn: float32 [768], P('shard')
- grad_rel_bias: float32 [32, 12], P('shard')
The draws below stay inside these ranges and needn't reach their ends.
Inputs may be any that keep to these rules, and one draw needn't show every extreme that they name: `segment_ids`: ids never fall along the bytes; a document holds 1 to 512 bytes. `buckets`: entry j - i + 511 is the bucket of key j seen from query i of one sequence.
All inputs are finite; a program needn't handle non-finite values.
Results may differ from the reference program's by a relative error of at most 0.019.
Values may be sent and summed in bfloat16 or wider, within the bound.
No kernel may reach another device: no remote copies, remote signals or barrier semaphores. Data moves between devices by JAX's collectives and lax.ppermute only.
A program may use at most 192 MiB of HBM per device.

```python
import math
import jax
import jax.numpy as jnp
import numpy as np
from jax import lax

D = 768
HEADS = 12
HD = 64
FF = 2048
NB = 32
TOK_DEV = 512
TOKENS = 16384
DEVICES = 32


def plant(drawn, own_key, least, top_value):
    dims = drawn.shape
    place = [jax.random.randint(jax.random.fold_in(own_key, axis), (), 0, dims[axis]) for axis in range(len(dims))]
    drawn = drawn.at[tuple(place)].set(least)
    longest = dims.index(max(dims))
    place[longest] = (place[longest] + 1) % dims[longest]
    return drawn.at[tuple(place)].set(top_value)


def steps_of(rng, shape, shards, least, top_value):
    factor_of = 1.0
    for dim, shards_of in shards:
        heights = jax.random.uniform(jax.random.fold_in(jax.random.fold_in(rng, 6), dim), (shards_of,), jnp.float32, least / len(shards), top_value / len(shards))
        factor_of = factor_of * jnp.repeat(jnp.exp(heights), shape[dim] // shards_of).reshape((-1,) + (1,) * (len(shape) - 1 - dim))
    return factor_of


def split_up(count, total, bound, lean):
    weights = [(1 << 20) // math.isqrt(rank ** lean) + 1 for rank in range(2, count + 1)]
    spare, counts = total - bound - (count - 1), [1] * (count - 1)
    while spare > 0:
        free = [i for i in range(count - 1) if counts[i] < bound]
        whole, remaining = sum([weights[i] for i in free]), spare
        for i in free:
            more = min(bound - counts[i], max(1, remaining * weights[i] // whole), spare)
            counts[i] = counts[i] + more
            spare = spare - more
    return np.array([bound] + counts)


def ragged(own_key, number_of, total, most, skew):
    if number_of == 2:
        one = jax.random.randint(own_key, (), max(1, total - most), min(most, total - 1) + 1)
        return jnp.stack([one, total - one])
    sizes = jnp.asarray(split_up(number_of, total, most, skew), jnp.int32)
    twos = (number_of - 1) // 2
    donor, receiver = sizes[1:1 + 2 * twos:2], sizes[2:2 + 2 * twos:2]
    slack = jnp.minimum(donor - 1, most - receiver)
    shifted = jax.random.randint(jax.random.fold_in(own_key, 1), (twos,), 0, 1 << 20) % (slack + 1)
    sizes = sizes.at[1:1 + 2 * twos:2].set(donor - shifted).at[2:2 + 2 * twos:2].set(receiver + shifted)
    return sizes[jax.random.permutation(jax.random.fold_in(own_key, 2), number_of)]


def noise(stream_key, extent, scale, reach, shards=(), kind=jnp.bfloat16):
    gain = steps_of(stream_key, extent, shards, -0.22, 0.18) if shards else 1.0
    values = jax.random.normal(stream_key, extent, jnp.float32) * scale * gain
    return jnp.minimum(jnp.maximum(values, -reach), reach).astype(kind)


def setup_inputs(seed: int = 0) -> dict:
    key_of = jax.random.split(jax.random.key(seed), 15)
    tokens = noise(key_of[0], (TOKENS, D), 1.0, 6.0, ((0, 32),))
    segment_ids = jnp.searchsorted(jnp.cumsum(ragged(key_of[1], 16 * DEVICES, TOKENS, TOK_DEV, 2)), jnp.arange(TOKENS), side="right").astype(jnp.int32)
    buckets = plant(jax.random.randint(key_of[2], (2 * TOK_DEV - 1,), 0, NB), jax.random.fold_in(key_of[2], 1), 0, NB - 1).astype(jnp.int32)
    w_query = noise(key_of[3], (D, D), D ** -0.5, 0.21875, ((0, 8),))
    w_key = noise(key_of[4], (D, D), D ** -0.5, 0.21875, ((0, 8),))
    w_value = noise(key_of[5], (D, D), D ** -0.5, 0.21875, ((0, 8),))
    w_output = noise(key_of[6], (D, D), (D // 8) ** -0.5, 0.625, ((0, 8),))
    w_gate = noise(key_of[7], (D, FF), D ** -0.5, 0.21875, ((0, 8),))
    w_up = noise(key_of[8], (D, FF), D ** -0.5, 0.21875, ((0, 8),))
    w_down = noise(key_of[9], (FF, D), FF ** -0.5, 0.125, ((0, 8),))
    norm_attn = jnp.clip(1.0 + 0.18 * jax.random.normal(key_of[10], (D,), jnp.float32), 0.099609375, 1.8984375).astype(jnp.bfloat16)
    norm_ffn = jnp.clip(1.0 + 0.18 * jax.random.normal(key_of[11], (D,), jnp.float32), 0.099609375, 1.8984375).astype(jnp.bfloat16)
    rel_bias = noise(key_of[12], (NB, HEADS), 1.0, 4.0, ((0, 8),))
    cotangent = noise(key_of[13], (TOKENS, D), 1.0, 6.0, ((0, 32),))
    return dict(tokens=tokens, segment_ids=segment_ids, buckets=buckets, w_query=w_query, w_key=w_key, w_value=w_value, w_output=w_output, w_gate=w_gate, w_up=w_up, w_down=w_down, norm_attn=norm_attn, norm_ffn=norm_ffn, rel_bias=rel_bias, cotangent=cotangent)


EPSILON = 1e-06
HIGHEST = lax.Precision.HIGHEST

@jax.custom_vjp
def low(v):
    return lax.optimization_barrier(v.astype(jnp.bfloat16)).astype(jnp.float32)

@jax.custom_vjp
def low_back(v):
    return v

def low_keep(v):
    return (low(v), None)

def low_pass(kept, grad):
    return (grad,)

def back_keep(v):
    return (v, None)

def back_low(kept, grad):
    return (low(grad),)
low.defvjp(low_keep, low_pass)
low_back.defvjp(back_keep, back_low)

def matmul_hi(left_op, right_op):
    return jnp.dot(left_op, right_op, precision=HIGHEST, preferred_element_type=jnp.float32)

def rms_norm(values, gain_vec):
    return values * lax.rsqrt(lax.optimization_barrier(jnp.mean(values * values, axis=-1, keepdims=True)) + EPSILON) * gain_vec

def encoder_layer(tokens, w_query, w_key, w_value, w_output, w_gate, w_up, w_down, norm_attn, norm_ffn, rel_bias, segment_ids, buckets):
    normed_one = low(rms_norm(tokens, norm_attn))
    queries = low(low_back(matmul_hi(normed_one, w_query)))
    key_rows = low(low_back(matmul_hi(normed_one, w_key)))
    value_rows = low(low_back(matmul_hi(normed_one, w_value)))
    offsets_bias = rel_bias[buckets].T
    position = jnp.arange(TOK_DEV, dtype=jnp.int32)
    offset = position[None, :] - position[:, None] + (TOK_DEV - 1)
    rel_terms = offsets_bias[:, offset]

    def sequence(inputs):
        query_seq, key_seq, value_seq, segment_seq = inputs
        scores = jnp.einsum('qhd,khd->hqk', query_seq, key_seq, precision=HIGHEST) * HD ** (-0.5) + rel_terms
        same_doc = segment_seq[:, None] == segment_seq[None, :]
        scores = low_back(jnp.where(same_doc[None], scores, -1000000000.0))
        row_peak = lax.optimization_barrier(jnp.max(scores, axis=-1, keepdims=True))
        weights_exp = jnp.exp(scores - row_peak)
        prob_rows = low(weights_exp / lax.optimization_barrier(jnp.sum(weights_exp, axis=-1, keepdims=True)))
        return jnp.einsum('hqk,khd->qhd', prob_rows, value_seq, precision=HIGHEST)
    seq_count = TOKENS // TOK_DEV
    attended = lax.map(jax.checkpoint(sequence), (queries.reshape(seq_count, TOK_DEV, HEADS, HD), key_rows.reshape(seq_count, TOK_DEV, HEADS, HD), value_rows.reshape(seq_count, TOK_DEV, HEADS, HD), segment_ids.reshape(seq_count, TOK_DEV)))
    attended = low(low_back(attended.reshape(TOKENS, D)))
    middle = tokens + low_back(matmul_hi(attended, w_output))
    normed_two = low(rms_norm(middle, norm_ffn))
    gate_pre = low_back(matmul_hi(normed_two, w_gate))
    up_part = low_back(matmul_hi(normed_two, w_up))
    hidden = low(jax.nn.gelu(gate_pre, approximate=True) * up_part)
    return middle + low_back(matmul_hi(hidden, w_down))

def reference(tokens, segment_ids, buckets, w_query, w_key, w_value, w_output, w_gate, w_up, w_down, norm_attn, norm_ffn, rel_bias, cotangent):

    def closed(tok_f, query_f, key_f, value_f, output_f, gate_f, up_f, down_f, attn_gain, ffn_gain, bias_f):
        return encoder_layer(tok_f, query_f, key_f, value_f, output_f, gate_f, up_f, down_f, attn_gain, ffn_gain, bias_f, segment_ids, buckets)
    result, pullback = jax.vjp(closed, tokens.astype(jnp.float32), w_query.astype(jnp.float32), w_key.astype(jnp.float32), w_value.astype(jnp.float32), w_output.astype(jnp.float32), w_gate.astype(jnp.float32), w_up.astype(jnp.float32), w_down.astype(jnp.float32), norm_attn.astype(jnp.float32), norm_ffn.astype(jnp.float32), rel_bias.astype(jnp.float32))
    gradients = pullback(cotangent.astype(jnp.float32))
    return (result.astype(jnp.bfloat16), gradients[0].astype(jnp.bfloat16), gradients[1], gradients[2], gradients[3], gradients[4], gradients[5], gradients[6], gradients[7], gradients[8], gradients[9], gradients[10])
```

```python
import functools

import jax
import jax.numpy as jnp
from jax import lax
from jax.experimental import pallas as pl
from jax.experimental.pallas import tpu as pltpu
from jax.sharding import PartitionSpec as P

bf16 = jnp.bfloat16
f32 = jnp.float32
EPS = 1e-06
SCALE = 0.125
MASKED = -1000000000.0
VMEM_LIMIT = 63 * 1024 * 1024
NT = (((1,), (1,)), ((), ()))
NN = (((1,), (0,)), ((), ()))


def mm(a, b, dims=NN):
    return lax.dot_general(a, b, dims, preferred_element_type=f32)


def whole(shape):
    zeros = (0,) * len(shape)
    return pl.BlockSpec(shape, lambda *_: zeros)


ANY = pl.BlockSpec(memory_space=pl.ANY)
SMEM = pl.BlockSpec(memory_space=pltpu.SMEM)


class Cut:
    def __init__(self, zn, yn, xn, xsplit):
        self.zn, self.yn, self.xn, self.nx = zn, yn, xn, (xn if xsplit else 1)

    def count(self):
        return 2 * self.nx * self.yn

    def start(self, ids, refs, piece, place, sem, cos=(0, 1)):
        z, y, x = ids[0], ids[1], ids[2]
        for co in cos:
            for xo in range(self.nx):
                for yo in range(self.yn):
                    ref = refs[(co * self.nx + xo) * self.yn + yo]
                    for k in range(self.zn):
                        zz = lax.rem(z - k + self.zn, self.zn)
                        yy = lax.rem(y + yo, self.yn)
                        block = zz * self.yn + yy
                        row = block if self.nx == 1 else block * self.nx + lax.rem(x + xo, self.nx)
                        for source, target in zip(piece(ref, k), place(co, row)):
                            pltpu.make_async_copy(source, target, sem).start()


def drain(target, sem):
    pltpu.make_async_copy(target, target, sem).wait()


def toeplitz_kernel(rel_ref, hot_ref, out_ref, line):
    heads, kinds = out_ref.shape[0], out_ref.shape[1]

    @pl.when(pl.program_id(0) == 0)
    def _():
        rel = rel_ref[...][:, :32].astype(bf16)
        line[...] = mm(rel, hot_ref[...])

    length = 512
    for h in range(heads):
        head = pl.program_id(0) * heads + h
        for kind in range(kinds):
            d = kind - kinds // 2
            start = length - 128 * d - 128
            spread = jnp.broadcast_to(line[pl.ds(head, 1), start:start + 256], (128, 256))
            out_ref[h, kind] = pltpu.roll(spread, 129, 1, stride=1, stride_axis=0)[:, :128]


def toeplitz(rel_rows, hot_rev):
    return pl.pallas_call(
        toeplitz_kernel,
        grid=(6,),
        in_specs=[whole(rel_rows.shape), whole(hot_rev.shape)],
        out_specs=pl.BlockSpec((2, 7, 128, 128), lambda j: (j, 0, 0, 0)),
        out_shape=jax.ShapeDtypeStruct((12, 7, 128, 128), f32),
        scratch_shapes=[pltpu.VMEM((16, 1024), f32)],
        compiler_params=pltpu.CompilerParams(vmem_limit_bytes=VMEM_LIMIT),
        name="toeplitz",
    )(rel_rows, hot_rev)


def gains(small, row):
    return jnp.concatenate([small[row:row + 1, :], small[row + 1:row + 2, :]], axis=1)


def attend_kernel(cut, ids, tok, small, segc, segr, toep, *rest):
    chunks, rest = rest[: cut.count()], rest[cut.count():]
    n1_ref, n1t_ref, q_ref, k_ref, v_ref, o_ref, ot_ref, pt_ref, w_ref, mask_ref, sem = rest
    length = tok.shape[0]
    nb = length // 128

    @pl.when(pl.program_id(0) == 0)
    def _():
        rows = 48

        def piece(ref, k):
            return [ref.at[k, rows * i:rows * i + rows, :] for i in range(3)]

        def place(co, row):
            cc = lax.rem(ids[3] + co, 2)
            return [w_ref.at[i, cc, pl.ds(pl.multiple_of(row * rows, 16), rows), :] for i in range(3)]

        cut.start(ids, chunks, piece, place, sem)
        for i in range(nb):
            block = pl.ds(128 * i, 128)
            x = tok[block, :].astype(f32)
            inverse = lax.rsqrt(jnp.mean(x * x, axis=-1, keepdims=True) + EPS)
            n1_ref[block, :] = (x * inverse * gains(small, 12)).astype(bf16)
            same = segc[block, :] == segr[...]
            mask_ref[block, :] = jnp.where(same, 0.0, MASKED)
            n1t_ref[:, block] = n1_ref[block, :].T
        drain(w_ref, sem)
        for cc in range(2):
            col = slice(384 * cc, 384 * cc + 384)
            for i in range(2):
                block = slice(256 * i, 256 * i + 256)
                n1 = n1_ref[block, :]
                q_ref[block, col] = (mm(n1, w_ref[0, cc]) * SCALE).astype(bf16)
                k_ref[block, col] = mm(n1, w_ref[1, cc]).astype(bf16)
                v_ref[block, col] = mm(n1, w_ref[2, cc]).astype(bf16)

    col = pl.ds(pl.multiple_of(pl.program_id(0) * 128, 128), 128)
    q2, k2, v2 = q_ref[:, col], k_ref[:, col], v_ref[:, col]
    v2t = v2.T
    lane = lax.broadcasted_iota(jnp.int32, (1, 128), 1)
    halves = []
    for a in range(2):
        mine = (lane < 64) if a == 0 else (lane >= 64)
        qm = jnp.where(mine, q2, jnp.zeros_like(q2))
        for qb in range(nb):
            qs = qm[128 * qb:128 * qb + 128]
            scores = []
            for kb in range(nb):
                s = mm(k2[128 * kb:128 * kb + 128], qs, NT)
                s = s + toep[a, kb - qb + nb - 1] + mask_ref[128 * kb:128 * kb + 128, 128 * qb:128 * qb + 128]
                scores.append(s)
            peak = functools.reduce(jnp.maximum, scores)
            peak = jnp.max(peak, axis=0, keepdims=True)
            scores = [jnp.exp(s - peak) for s in scores]
            total = jnp.sum(functools.reduce(jnp.add, scores), axis=0, keepdims=True)
            inverse = 1.0 / total
            for kb in range(nb):
                pt_ref[a, 128 * kb:128 * kb + 128, 128 * qb:128 * qb + 128] = (scores[kb] * inverse).astype(bf16)
        halves.append(mm(v2t[64 * a:64 * a + 64], pt_ref[a]))
    ot = jnp.concatenate(halves, axis=0).astype(bf16)
    ot_ref[...] = ot
    o_ref[...] = ot.T


def attend(cut, ids, tok, small, segc, segr, toep, chunks):
    length = tok.shape[0]
    full = jax.ShapeDtypeStruct((length, 768), bf16)
    flip = jax.ShapeDtypeStruct((768, length), bf16)
    wide = whole((length, 768))
    return pl.pallas_call(
        functools.partial(attend_kernel, cut),
        grid=(6,),
        in_specs=[SMEM, wide, whole(small.shape), whole(segc.shape), whole(segr.shape),
                  pl.BlockSpec((2, 7, 128, 128), lambda j: (j, 0, 0, 0))] + [ANY] * len(chunks),
        out_specs=[wide, whole((768, length)), wide, wide, wide,
                   pl.BlockSpec((length, 128), lambda j: (0, j)),
                   pl.BlockSpec((128, length), lambda j: (j, 0)),
                   pl.BlockSpec((2, length, length), lambda j: (j, 0, 0))],
        out_shape=[full, flip, full, full, full, full, flip,
                   jax.ShapeDtypeStruct((12, length, length), bf16)],
        scratch_shapes=[pltpu.VMEM((3, 2, 768, 384), bf16), pltpu.VMEM((length, length), f32),
                        pltpu.SemaphoreType.DMA],
        compiler_params=pltpu.CompilerParams(vmem_limit_bytes=VMEM_LIMIT),
        cost_estimate=pl.CostEstimate(flops=3_500_000_000, bytes_accessed=20_000_000, transcendentals=3_145_728),
        name="attend",
    )(ids, tok, small, segc, segr, toep, *chunks)


def load_output(cut, ids, chunks, wo_ref, sem):
    rows = 48

    def piece(ref, k):
        return [ref.at[k, 128:176, :]]

    def place(co, row):
        return [wo_ref.at[co, pl.ds(pl.multiple_of(row * rows, 16), rows), :]]

    cut.start(ids, chunks, piece, place, sem)


def project_kernel(cut, ids, tok, small, o, *rest):
    chunks, rest = rest[: cut.count()], rest[cut.count():]
    x1_ref, n2_ref, n2t_ref, wo_ref, sem = rest
    load_output(cut, ids, chunks, wo_ref, sem)
    drain(wo_ref, sem)
    c = ids[3]
    flip = c == 1
    for i in range(2):
        block = slice(256 * i, 256 * i + 256)
        own = mm(o[block, :], wo_ref[0])
        other = mm(o[block, :], wo_ref[1])
        left = jnp.where(flip, other, own)
        right = jnp.where(flip, own, other)
        x1 = tok[block, :].astype(f32) + jnp.concatenate([left, right], axis=1)
        x1_ref[block, :] = x1
        inverse = lax.rsqrt(jnp.mean(x1 * x1, axis=-1, keepdims=True) + EPS)
        n2 = (x1 * inverse * gains(small, 14)).astype(bf16)
        n2_ref[block, :] = n2
        n2t_ref[:, block] = n2.T


def project(cut, ids, tok, small, o, chunks):
    length = tok.shape[0]
    wide = whole((length, 768))
    return pl.pallas_call(
        functools.partial(project_kernel, cut),
        grid=(1,),
        in_specs=[SMEM, wide, whole(small.shape), wide] + [ANY] * len(chunks),
        out_specs=[wide, wide, whole((768, length))],
        out_shape=[jax.ShapeDtypeStruct((length, 768), f32), jax.ShapeDtypeStruct((length, 768), bf16),
                   jax.ShapeDtypeStruct((768, length), bf16)],
        scratch_shapes=[pltpu.VMEM((2, 768, 384), bf16), pltpu.SemaphoreType.DMA],
        compiler_params=pltpu.CompilerParams(vmem_limit_bytes=VMEM_LIMIT),
        cost_estimate=pl.CostEstimate(flops=604_000_000, bytes_accessed=6_000_000, transcendentals=0),
        name="project",
    )(ids, tok, small, o, *chunks)


ROOT = 0.7978845608028654
CUBIC = 0.044715


def ffn_kernel(cuts, co, first, ids, n2, n2t, cot, *rest):
    cut_g, cut_u, cut_d = cuts
    ng, nu, nd = (c.nx * c.yn for c in cuts)
    g_chunks, rest = rest[:ng], rest[ng:]
    u_chunks, rest = rest[:nu], rest[nu:]
    d_chunks, rest = rest[:nd], rest[nd:]
    if not first:
        out_in, dn2_in, rest = rest[0], rest[1], rest[2:]
    dg_ref, du_ref, dd_ref, out_ref, dn2_ref, wg, wu, wd, h_s, a_s, b_s, sems = rest
    j = pl.program_id(0)
    width = dg_ref.shape[1]

    @pl.when(j == 0)
    def _():
        for cut, chunks, target, sem in ((cut_g, g_chunks, wg, sems.at[0]), (cut_u, u_chunks, wu, sems.at[1])):
            rows = 96 // cut.nx

            def piece(ref, k):
                return [ref.at[k]]

            def place(_, row, target=target, rows=rows):
                return [target.at[pl.ds(pl.multiple_of(row * rows, 16), rows), :]]

            cut.start(ids, chunks, piece, place, sem, (0,))
        rows = 128 // cut_d.nx

        def piece_d(ref, k):
            return [ref.at[k, 0:rows, :], ref.at[k, rows:2 * rows, :]]

        def place_d(_, row):
            at = pl.ds(pl.multiple_of(row * rows, 16), rows)
            return [wd.at[at, 0:384], wd.at[at, 384:768]]

        cut_d.start(ids, d_chunks, piece_d, place_d, sems.at[2], (0,))
        if first:
            out_ref[...] = jnp.zeros_like(out_ref)
            dn2_ref[...] = jnp.zeros_like(dn2_ref)
        else:
            out_ref[...] = out_in[...]
            dn2_ref[...] = dn2_in[...]
        drain(wg, sems.at[0])
        drain(wu, sems.at[1])
        drain(wd, sems.at[2])

    tile = pl.ds(pl.multiple_of(j * width, width), width)
    wgt, wut, wdt = wg[:, tile], wu[:, tile], wd[tile, :]
    for i in range(2):
        block = slice(256 * i, 256 * i + 256)
        rows = n2[block, :]
        gate = mm(rows, wgt)
        up = mm(rows, wut)
        dh = mm(cot[block, :], wdt, NT)
        square = gate * gate
        t = jnp.tanh(ROOT * (gate + CUBIC * square * gate))
        half = 0.5 * (1.0 + t)
        act = gate * half
        slope = half + 0.5 * gate * (1.0 - t * t) * (ROOT * (1.0 + 3.0 * CUBIC * square))
        h = (act * up).astype(bf16)
        dgate = (dh * up * slope).astype(bf16)
        dup = (dh * act).astype(bf16)
        h_s[block, :] = h
        a_s[block, :] = dgate
        b_s[block, :] = dup
        out_ref[block, :] += mm(h, wdt)
        dn2_ref[block, :] += mm(dgate, wgt, NT) + mm(dup, wut, NT)
    dg_ref[...] = mm(n2t[...], a_s[...]).astype(bf16)
    du_ref[...] = mm(n2t[...], b_s[...]).astype(bf16)
    dd = mm(h_s[...].T, cot[...]).astype(bf16)
    part = 64
    for b in range(width // part):
        dd_ref[b, 0:part, :] = dd[part * b:part * b + part, 0:384]
        dd_ref[b, part:2 * part, :] = dd[part * b:part * b + part, 384:768]


def ffn(cuts, co, ids, n2, n2t, cot, g_chunks, u_chunks, d_chunks, carried):
    length = n2.shape[0]
    first = carried is None
    width = 256
    wide = whole((length, 768))
    carried = () if first else tuple(carried)
    pick = [list(c)[co * len(c) // 2:(co + 1) * len(c) // 2] for c in (g_chunks, u_chunks, d_chunks)]
    chunks = pick[0] + pick[1] + pick[2]
    total = jax.ShapeDtypeStruct((length, 768), f32)
    return pl.pallas_call(
        functools.partial(ffn_kernel, cuts, co, first),
        grid=(1024 // width,),
        in_specs=[SMEM, wide, whole((768, length)), wide] + [ANY] * len(chunks) + [wide] * len(carried),
        out_specs=[pl.BlockSpec((768, width), lambda j: (0, j)), pl.BlockSpec((768, width), lambda j: (0, j)),
                   pl.BlockSpec((width // 64, 128, 384), lambda j: (j, 0, 0)), wide, wide],
        out_shape=[jax.ShapeDtypeStruct((768, 1024), bf16), jax.ShapeDtypeStruct((768, 1024), bf16),
                   jax.ShapeDtypeStruct((16, 128, 384), bf16), total, total],
        scratch_shapes=[pltpu.VMEM((768, 1024), bf16), pltpu.VMEM((768, 1024), bf16), pltpu.VMEM((1024, 768), bf16),
                        pltpu.VMEM((length, width), bf16), pltpu.VMEM((length, width), bf16),
                        pltpu.VMEM((length, width), bf16), pltpu.SemaphoreType.DMA((3,))],
        compiler_params=pltpu.CompilerParams(vmem_limit_bytes=VMEM_LIMIT),
        cost_estimate=pl.CostEstimate(flops=7_250_000_000, bytes_accessed=16_000_000, transcendentals=524_288),
        name="ffn",
    )(ids, n2, n2t, cot, *chunks, *carried)


def middle_kernel(cut, ids, x1_ref, out_acc, dn2, cot, ot, small, *rest):
    chunks, rest = rest[: cut.count()], rest[cut.count():]
    out_ref, dx1_ref, do_ref, own_ref, other_ref, wo_ref, da_s, sem = rest
    load_output(cut, ids, chunks, wo_ref, sem)
    nb = x1_ref.shape[0] // 128
    c = ids[3]
    for i in range(nb):
        block = slice(128 * i, 128 * i + 128)
        x1 = x1_ref[block, :]
        out_ref[block, :] = (x1 + out_acc[block, :]).astype(bf16)
        inverse = lax.rsqrt(jnp.mean(x1 * x1, axis=-1, keepdims=True) + EPS)
        u = x1 * inverse
        e = dn2[block, :] * gains(small, 14)
        dx1 = cot[block, :].astype(f32) + inverse * (e - u * jnp.mean(e * u, axis=-1, keepdims=True))
        dx1_ref[block, :] = dx1
        da = dx1.astype(bf16)
        da_s[0, block, :] = da[:, :384]
        da_s[1, block, :] = da[:, 384:]
    drain(wo_ref, sem)
    for co, target in ((1, other_ref), (0, own_ref)):
        da = da_s[lax.rem(c + co, 2)]
        grad = mm(ot[...], da).astype(bf16)
        for b in range(16):
            target[b] = grad[48 * b:48 * b + 48, :]
    for i in range(2):
        block = pl.ds(256 * i, 256)
        do = mm(da_s[c, block, :], wo_ref[0], NT) + mm(da_s[1 - c, block, :], wo_ref[1], NT)
        do_ref[block, :] = do.astype(bf16)


def middle(cut, ids, x1, out_acc, dn2, cot, ot, small, chunks):
    length = x1.shape[0]
    wide = whole((length, 768))
    half = jax.ShapeDtypeStruct((16, 48, 384), bf16)
    return pl.pallas_call(
        functools.partial(middle_kernel, cut),
        grid=(1,),
        in_specs=[SMEM, wide, wide, wide, wide, whole((768, length)), whole(small.shape)] + [ANY] * len(chunks),
        out_specs=[wide, wide, wide, whole(half.shape), whole(half.shape)],
        out_shape=[jax.ShapeDtypeStruct((length, 768), bf16), jax.ShapeDtypeStruct((length, 768), f32),
                   jax.ShapeDtypeStruct((length, 768), bf16), half, half],
        scratch_shapes=[pltpu.VMEM((2, 768, 384), bf16), pltpu.VMEM((2, length, 384), bf16),
                        pltpu.SemaphoreType.DMA],
        compiler_params=pltpu.CompilerParams(vmem_limit_bytes=VMEM_LIMIT),
        cost_estimate=pl.CostEstimate(flops=1_208_000_000, bytes_accessed=12_000_000, transcendentals=0),
        name="middle",
    )(ids, x1, out_acc, dn2, cot, ot, small, *chunks)


def attend_back_kernel(half_ref, q, k, v, do, o, pt, n1t, hot, dq_ref, dk_ref, dv_ref, pack_ref, ds_s, diag, sums):
    j = pl.program_id(0)
    length = q.shape[0]
    nb = length // 128
    kinds = 2 * nb - 1
    q2, k2, v2, do2 = q[...], k[...], v[...], do[...]
    lane = lax.broadcasted_iota(jnp.int32, (1, 128), 1)
    k2t = k2.T
    inner = do2.astype(f32) * o[...].astype(f32)
    high = inner.astype(bf16)
    low = (inner - high.astype(f32)).astype(bf16)
    ones = jnp.ones((8, 128), bf16)
    dk = jnp.zeros((length, 128), f32)
    dv = jnp.zeros((length, 128), f32)
    dqs = []
    lane8 = lax.broadcasted_iota(jnp.int32, (8, 128), 1)
    sub8 = lax.broadcasted_iota(jnp.int32, (8, 128), 0)
    size = 16 * kinds
    row_of = lax.broadcasted_iota(jnp.int32, (size, size), 0)
    col_of = lax.broadcasted_iota(jnp.int32, (size, size), 1)
    swap = ((row_of >> 3 == col_of >> 3) & ((row_of & 7) + (col_of & 7) == 7)).astype(f32)
    for a in range(2):
        mine = (lane < 64) if a == 0 else (lane >= 64)
        zero = jnp.zeros_like(q2)
        qm = jnp.where(mine, q2, zero)
        dom = jnp.where(mine, do2, zero)
        weight = jnp.where(mine, ones, jnp.zeros_like(ones))
        line = (mm(weight, high, NT) + mm(weight, low, NT))[0:1, :]
        for qb in range(nb):
            cols = slice(128 * qb, 128 * qb + 128)
            for kb in range(nb):
                rows = slice(128 * kb, 128 * kb + 128)
                dp = mm(v2[rows], dom[cols], NT)
                ds = pt[a, rows, cols].astype(f32) * (dp - line[:, cols])
                ds_s[a, rows, cols] = ds.astype(bf16)
                kind = kb - qb + nb - 1
                if qb == 0 or kb == 0:
                    diag[kind] = ds
                else:
                    diag[kind] += ds
        dqs.append(mm(k2t[64 * a:64 * a + 64], ds_s[a]) * SCALE)
        dk = dk + mm(ds_s[a], qm)
        dv = dv + mm(pt[a], dom)
        groups = []
        for kind in range(kinds):
            upper, every = jnp.zeros((8, 128), f32), jnp.zeros((8, 128), f32)
            for g in range(16):
                part = diag[kind, 8 * g:8 * g + 8, :]
                if g:
                    part = pltpu.roll(part, 128 - 8 * g, 1)
                every = every + part
                upper = upper + jnp.where(((lane8 + 8 * g) & 127) >= sub8 + 8 * g, part, 0.0)
            groups += [upper, every - upper]
        flipped = lax.dot_general(swap, jnp.concatenate(groups, axis=0), NN, precision=lax.Precision.HIGHEST,
                                  preferred_element_type=f32)
        for r in range(2 * kinds):
            rolled = pltpu.roll(flipped[8 * r:8 * r + 8], 121, 1, stride=1, stride_axis=0)
            sums[r, pl.ds(2 * j + a, 1), :] = jnp.sum(rolled, axis=0, keepdims=True)
    col = pl.ds(pl.multiple_of(128 * j, 128), 128)
    dq_ref[:, col] = jnp.concatenate(dqs, axis=0).astype(bf16).T
    dk_ref[:, col] = dk.astype(bf16)
    dv_ref[:, col] = dv.astype(bf16)

    @pl.when(j == 2)
    def _():
        table = jnp.zeros((8, 128), f32)
        for r in range(2 * kinds):
            table = table + lax.dot_general(sums[r], hot[r], NN, precision=lax.Precision.HIGHEST,
                                            preferred_element_type=f32)
        keep = lax.broadcasted_iota(jnp.int32, (8, 128), 0) < 6
        tail = jnp.concatenate([jnp.where(keep, table, 0.0), jnp.zeros((8, 256), f32)], axis=1)
        tail = jnp.concatenate([tail, jnp.zeros((8, 384), f32)], axis=0).astype(bf16)
        for i, part in enumerate((dq_ref, dk_ref, dv_ref)):
            grad = mm(n1t[...], part[...]).astype(bf16)
            for b in range(16):
                pack_ref[b, 48 * i:48 * i + 48, :] = grad[48 * b:48 * b + 48, :]
        for b in range(16):
            pack_ref[b, 144:160, :] = tail


def attend_back(half, q, k, v, do, o, pt, n1t, hot):
    length = q.shape[0]
    strip = pl.BlockSpec((length, 128), lambda j, h: (0, 3 * h[0] + j))
    part = jax.ShapeDtypeStruct((length, 384), bf16)
    keep = pl.BlockSpec((length, 384), lambda j, h: (0, 0))
    kinds = 2 * (length // 128) - 1
    return pl.pallas_call(
        attend_back_kernel,
        grid_spec=pltpu.PrefetchScalarGridSpec(
            num_scalar_prefetch=1,
            grid=(3,),
            in_specs=[strip, strip, strip, strip, strip,
                      pl.BlockSpec((2, length, length), lambda j, h: (3 * h[0] + j, 0, 0)),
                      whole((768, length)), whole(hot.shape)],
            out_specs=[keep, keep, keep, pl.BlockSpec((16, 160, 384), lambda j, h: (0, 0, 0))],
            scratch_shapes=[pltpu.VMEM((2, length, length), bf16), pltpu.VMEM((kinds, 128, 128), f32),
                            pltpu.VMEM((2 * kinds, 8, 128), f32)],
        ),
        out_shape=[part, part, part, jax.ShapeDtypeStruct((16, 160, 384), bf16)],
        compiler_params=pltpu.CompilerParams(vmem_limit_bytes=VMEM_LIMIT),
        cost_estimate=pl.CostEstimate(flops=2_500_000_000, bytes_accessed=10_000_000, transcendentals=0),
        name="attend_back",
    )(half, q, k, v, do, o, pt, n1t, hot)


def first_kernel(cut, ids, tok, small, dx1, dq0, dk0, dv0, dq1, dk1, dv1, *rest):
    chunks, rest = rest[: cut.count()], rest[cut.count():]
    out_ref, w_ref, sem = rest
    rows = 48

    def piece(ref, k):
        return [ref.at[k, rows * i:rows * i + rows, :] for i in range(3)]

    def place(co, row):
        return [w_ref.at[i, co, pl.ds(pl.multiple_of(row * rows, 16), rows), :] for i in range(3)]

    cut.start(ids, chunks, piece, place, sem)
    drain(w_ref, sem)
    for i in range(tok.shape[0] // 128):
        block = slice(128 * i, 128 * i + 128)
        dn1 = None
        for co, parts in ((0, (dq0, dk0, dv0)), (1, (dq1, dk1, dv1))):
            for w in range(3):
                term = mm(parts[w][block, :], w_ref[w, co], NT)
                dn1 = term if dn1 is None else dn1 + term
        x = tok[block, :].astype(f32)
        inverse = lax.rsqrt(jnp.mean(x * x, axis=-1, keepdims=True) + EPS)
        u = x * inverse
        e = dn1 * gains(small, 12)
        out = dx1[block, :] + inverse * (e - u * jnp.mean(e * u, axis=-1, keepdims=True))
        out_ref[block, :] = out.astype(bf16)


def first(cut, ids, tok, small, dx1, parts, chunks):
    length = tok.shape[0]
    wide = whole((length, 768))
    return pl.pallas_call(
        functools.partial(first_kernel, cut),
        grid=(1,),
        in_specs=[SMEM, wide, whole(small.shape), wide] + [whole((length, 384))] * 6 + [ANY] * len(chunks),
        out_specs=wide,
        out_shape=jax.ShapeDtypeStruct((length, 768), bf16),
        scratch_shapes=[pltpu.VMEM((3, 2, 768, 384), bf16), pltpu.SemaphoreType.DMA],
        compiler_params=pltpu.CompilerParams(vmem_limit_bytes=VMEM_LIMIT),
        cost_estimate=pl.CostEstimate(flops=1_812_000_000, bytes_accessed=10_000_000, transcendentals=0),
        name="first",
    )(ids, tok, small, dx1, *parts, *chunks)


ZN, YN, XN = 4, 2, 2


def shift(value, axis, size, by=1):
    return lax.ppermute(value, axis, [(i, (i + by) % size) for i in range(size)])


def gather_group(pack, xsplit):
    far = {k: shift(pack, "z", ZN, k) for k in (1, ZN - 1, 2)}
    column = jnp.stack([pack] + [far[k] for k in range(1, ZN)])
    parts = [column, shift(column, "y", YN)]
    if xsplit:
        parts = parts + [shift(part, "x", XN) for part in parts]
    return parts + [shift(part, "c", 2) for part in parts]


def at(value, index, axis):
    return lax.dynamic_index_in_dim(value, index, axis, keepdims=False)


def scatter_group(own, swapped, xfirst, ids):
    z, y, x, _ = ids

    def both(index, axis):
        return at(own, index, axis).astype(f32) + at(swapped, index, axis).astype(f32)

    if xfirst:
        sent = shift(both(1 - x, 2).astype(bf16), "x", XN)
        mine = (both(x, 2) + sent.astype(f32)).astype(bf16)
        sent = shift(at(mine, 1 - y, 1), "y", YN)
        mine = (at(mine, y, 1).astype(f32) + sent.astype(f32)).astype(bf16)
    else:
        sent = shift(both(1 - y, 1).astype(bf16), "y", YN)
        mine = (both(y, 1) + sent.astype(f32)).astype(bf16)
    come = [shift(at(mine, (z + k) % ZN, 0), "z", ZN, k) for k in (1, ZN - 1, 2)]
    block = at(mine, z, 0).astype(f32)
    for part in come:
        block = block + part.astype(f32)
    block = block.astype(bf16)
    beside = shift(block, "x", XN)
    if xfirst:
        low, high = jnp.where(x == 0, block, beside), jnp.where(x == 0, beside, block)
        full = jnp.stack([low, high])
    else:
        full = (block.astype(f32) + beside.astype(f32)).astype(bf16)
    return full, shift(full, "c", 2)


def ordered(c, pair):
    return jnp.where(c == 0, pair[0], pair[1]), jnp.where(c == 0, pair[1], pair[0])


def fast(tokens, segment_ids, buckets, w_query, w_key, w_value, w_output, w_gate, w_up, w_down,
         norm_attn, norm_ffn, rel_bias, cotangent):
    ids = tuple(lax.axis_index(name).astype(jnp.int32) for name in ("z", "y", "x", "c"))
    z, y, x, c = ids
    b = z * YN + y
    places = jnp.stack(ids)
    length = tokens.shape[0]

    def corner(weight):
        return lax.dynamic_slice(weight, (x * 48, c * 384), (48, 384))

    zero = jnp.zeros((), jnp.int32)
    tail = jnp.zeros((12, 384), bf16)
    tail = lax.dynamic_update_slice(tail, rel_bias.T, (zero, b * 4))
    lines = jnp.zeros((2, 768), bf16)
    lines = lax.dynamic_update_slice(lines, jnp.stack([norm_attn, norm_ffn]), (zero, b * 96))
    tail = jnp.concatenate([tail, lines.reshape(4, 384)])
    pack_qkv = jnp.concatenate([corner(w_query), corner(w_key), corner(w_value), tail])
    pick = jnp.arange(8, dtype=jnp.int32)
    pack_g = at(w_gate.reshape(96, 8, 2, 128), c, 2).reshape(96, 1024)
    pack_u = at(at(w_up.reshape(2, 48, 8, 2, 128), c, 3), x, 0).reshape(48, 1024)
    down = at(w_down.reshape(2, 2, 64, 768), c, 0)
    down = at(down, x, 0)
    pack_d = jnp.concatenate([down[:, :384], down[:, 384:], corner(w_output)])

    qkv = gather_group(pack_qkv, True)
    gate = gather_group(pack_g, False)
    up = gather_group(pack_u, True)
    down = gather_group(pack_d, True)
    split, plain = Cut(ZN, YN, XN, True), Cut(ZN, YN, XN, False)

    small = (qkv[0][:, 144:160].astype(f32).sum(0) + qkv[1][:, 144:160].astype(f32).sum(0))
    kinds = jnp.arange(32, dtype=jnp.int32)
    flipped = jnp.pad(buckets[::-1], (0, 1))
    hot_rev = (flipped[None, :] == kinds[:, None]).astype(bf16)
    lane = jnp.arange(128, dtype=jnp.int32)
    offset = 128 * (jnp.arange(7, dtype=jnp.int32) - 3)[:, None, None] + jnp.array([0, 128], jnp.int32)[None, :, None]
    offset = offset - lane[None, None, :] + (length - 1)
    found = jnp.take(buckets, jnp.clip(offset, 0, 2 * length - 2).reshape(-1)).reshape(14, 128)
    hot = (found[:, :, None] == lane[None, None, :]).astype(f32)

    bias = toeplitz(small, hot_rev)
    n1, n1t, q, k, v, o, ot, pt = attend(
        split, places, tokens, small, segment_ids.reshape(length, 1), segment_ids.reshape(1, length), bias, qkv)
    x1, n2, n2t = project(split, places, tokens, small, o, down)
    cuts = (plain, split, split)
    other_g, other_u, other_d, acc, dn2 = ffn(cuts, 1, places, n2, n2t, cotangent, gate, up, down, None)
    come_g, come_u, come_d = (shift(a, "c", 2) for a in (other_g, other_u, other_d))
    own_g, own_u, own_d, acc, dn2 = ffn(cuts, 0, places, n2, n2t, cotangent, gate, up, down, (acc, dn2))
    output, dx1, do, own_o, other_o = middle(split, places, x1, acc, dn2, cotangent, ot, small, down)
    come_o = shift(other_o, "c", 2)

    wide = (ZN, YN, XN, 48, 1024)
    grad_g = scatter_group(own_g.reshape(wide), come_g.reshape(wide), True, ids)
    grad_u = scatter_group(own_u.reshape(wide), come_u.reshape(wide), False, ids)
    cut_d, cut_o = (ZN, YN, XN, 128, 384), (ZN, YN, XN, 48, 384)
    grad_d = scatter_group(jnp.concatenate([own_d.reshape(cut_d), own_o.reshape(cut_o)], axis=3),
                           jnp.concatenate([come_d.reshape(cut_d), come_o.reshape(cut_o)], axis=3), True, ids)

    dq1, dk1, dv1, other_q = attend_back((1 - c).reshape(1), q, k, v, do, o, pt, n1t, hot)
    come_q = shift(other_q, "c", 2)
    dq0, dk0, dv0, own_q = attend_back(c.reshape(1), q, k, v, do, o, pt, n1t, hot)
    cut_q = (ZN, YN, XN, 160, 384)
    own_q, come_q = own_q.reshape(cut_q), come_q.reshape(cut_q)
    grad_q = scatter_group(own_q[..., :80, :], come_q[..., :80, :], True, ids)
    grad_v = scatter_group(own_q[..., 80:, :], come_q[..., 80:, :], False, ids)
    grad_tokens = first(split, places, tokens, small, dx1, (dq0, dk0, dv0, dq1, dk1, dv1), qkv)

    left, right = ordered(c, [jnp.concatenate(pair, axis=1) for pair in zip(grad_q, grad_v)])
    both = jnp.concatenate([left, right], axis=-1).astype(f32)
    shares = [both[:, 48 * i:48 * i + 48].reshape(96, 768) for i in range(3)]
    rel = jnp.concatenate([left[0, 144:150, :32], right[0, 144:150, :32]]).astype(f32).T
    grad_rel = lax.dynamic_slice(rel, (b * 4, zero), (4, 12))
    left, right = ordered(c, grad_d)
    grad_w_output = jnp.concatenate([left[:, 128:], right[:, 128:]], axis=-1).astype(f32).reshape(96, 768)
    downs = [jnp.concatenate([part[:, :64], part[:, 64:128]], axis=-1).reshape(128, 768) for part in (left, right)]
    grad_w_down = jnp.concatenate(downs).astype(f32)
    wides = []
    for pair in (grad_g, grad_u):
        left, right = ordered(c, [part.reshape(96, 8, 1, 128) for part in pair])
        wides.append(jnp.concatenate([left, right], axis=2).astype(f32).reshape(96, 2048))

    def gain_grad(grads, weights, gain):
        total = sum((g * w.astype(f32)).sum(-1) for g, w in zip(grads, weights))
        return total / gain.astype(f32)

    grad_norm_attn = gain_grad(shares, (w_query, w_key, w_value), norm_attn)
    grad_norm_ffn = gain_grad(wides, (w_gate, w_up), norm_ffn)
    return (output, grad_tokens, shares[0], shares[1], shares[2], grad_w_output, wides[0], wides[1], grad_w_down,
            grad_norm_attn, grad_norm_ffn, grad_rel)


D = 768
HEADS = 12
HD = 64
NB = 32


EPSILON = 1e-06
HIGHEST = lax.Precision.HIGHEST


def product(left_op, right_op):
    return jnp.dot(left_op, right_op, preferred_element_type=jnp.float32)


def product_tn(left_op, right_op):
    return lax.dot_general(
        left_op, right_op, (((0,), (0,)), ((), ())), preferred_element_type=jnp.float32
    )


def product_nt(left_op, right_op):
    return lax.dot_general(
        left_op, right_op, (((1,), (1,)), ((), ())), preferred_element_type=jnp.float32
    )


def gelu_tanh(values):
    return jax.nn.gelu(values, approximate=True)


def normalize(values, gain_vec):
    inverse = lax.rsqrt(jnp.mean(values * values, axis=-1, keepdims=True) + EPSILON)
    return (values * inverse * gain_vec, inverse)


def normalize_back(grad_out, values, inverse, gain_vec):
    unit_rows = values * inverse
    grad_gain = jnp.sum(grad_out * unit_rows, axis=0)
    scaled = grad_out * gain_vec
    grad_in = inverse * (scaled - unit_rows * jnp.mean(scaled * unit_rows, axis=-1, keepdims=True))
    return (grad_in, grad_gain)


def toeplitz_rows(table_low, block_start, block_rows, length):
    heads = table_low.shape[0]
    padded = jnp.pad(table_low, ((0, 0), (0, 1)))
    tiled = jnp.broadcast_to(padded[:, None, :], (heads, block_rows, 2 * length))
    flat = tiled.reshape(heads, block_rows * 2 * length)[:, : block_rows * (2 * length - 1)]
    skewed = flat.reshape(heads, block_rows, 2 * length - 1)
    return lax.dynamic_slice_in_dim(skewed, length - 1 - block_start, length, 2)


def diagonal_sums(grad_low, block_start, length):
    heads, block_rows, unused_keys = grad_low.shape
    width = 2 * length - 1 + block_rows
    zero_index = jnp.zeros((), jnp.int32)
    placed = lax.dynamic_update_slice(
        jnp.zeros((heads, block_rows, width), jnp.bfloat16),
        grad_low,
        (zero_index, zero_index, length - 1 - block_start),
    )
    flat = jnp.pad(placed.reshape(heads, block_rows * width), ((0, 0), (0, block_rows)))
    sheared = flat.reshape(heads, block_rows, width + 1)[:, :, : 2 * length - 1]
    return jnp.sum(sheared, axis=1, dtype=jnp.float32)


def block_scores(query_block, segment_block, block_start, key_rows, segment_ids, table_low):
    block_rows = query_block.shape[0]
    length = key_rows.shape[0]
    raw_scores = jnp.einsum(
        "qhd,khd->hqk", query_block, key_rows, preferred_element_type=jnp.float32
    ) * HD ** (-0.5)
    rel_terms = toeplitz_rows(table_low, block_start, block_rows, length)
    same_doc = segment_block[:, None] == segment_ids[None, :]
    return jnp.where(same_doc[None], raw_scores + rel_terms.astype(jnp.float32), -1000000000.0)


def block_inputs(queries, segment_ids):
    length = queries.shape[0]
    block_rows = min(512, length)
    block_count = length // block_rows
    return (
        queries.reshape(block_count, block_rows, HEADS, HD),
        segment_ids.reshape(block_count, block_rows),
        jnp.arange(block_count, dtype=jnp.int32) * block_rows,
    )


def forward(weights, tokens_f, segment_ids, buckets):
    (
        query_full,
        key_full,
        value_full,
        output_full,
        gate_full,
        up_full,
        down_full,
        attn_gain,
        ffn_gain,
        bias_full,
    ) = weights
    length = tokens_f.shape[0]
    normed_one, inverse_one = normalize(tokens_f, attn_gain.astype(jnp.float32))
    normed_one = normed_one.astype(jnp.bfloat16)
    queries = product(normed_one, query_full).astype(jnp.bfloat16).reshape(length, HEADS, HD)
    key_rows = product(normed_one, key_full).astype(jnp.bfloat16).reshape(length, HEADS, HD)
    value_rows = product(normed_one, value_full).astype(jnp.bfloat16).reshape(length, HEADS, HD)
    bucket_onehot = (buckets[:, None] == jnp.arange(NB, dtype=jnp.int32)[None, :]).astype(
        jnp.bfloat16
    )
    table_low = product(bucket_onehot, bias_full).T.astype(jnp.bfloat16)

    def attend(inputs):
        query_block, segment_block, block_start = inputs
        scores = block_scores(
            query_block, segment_block, block_start, key_rows, segment_ids, table_low
        )
        row_peak = jnp.max(scores, axis=-1, keepdims=True)
        weights_exp = jnp.exp(scores - row_peak)
        row_total = jnp.sum(weights_exp, axis=-1, keepdims=True)
        prob_rows = (weights_exp / row_total).astype(jnp.bfloat16)
        block_out = jnp.einsum(
            "hqk,khd->qhd", prob_rows, value_rows, preferred_element_type=jnp.float32
        )
        return (block_out.astype(jnp.bfloat16), row_peak + jnp.log(row_total))

    attended, log_total = lax.map(attend, block_inputs(queries, segment_ids))
    attended = attended.reshape(length, D)
    middle = tokens_f + product(attended, output_full)
    normed_two, inverse_two = normalize(middle, ffn_gain.astype(jnp.float32))
    normed_two = normed_two.astype(jnp.bfloat16)
    gate_pre = product(normed_two, gate_full)
    up_part = product(normed_two, up_full)
    hidden = (gelu_tanh(gate_pre) * up_part).astype(jnp.bfloat16)
    output = middle + product(hidden, down_full)
    kept_acts = (
        normed_one,
        inverse_one,
        queries,
        key_rows,
        value_rows,
        table_low,
        attended,
        log_total,
        middle,
        normed_two,
        inverse_two,
        gate_pre,
        up_part,
        hidden,
    )
    return (output, kept_acts)


def shards(
    tokens,
    segment_ids,
    buckets,
    w_query,
    w_key,
    w_value,
    w_output,
    w_gate,
    w_up,
    w_down,
    norm_attn,
    norm_ffn,
    rel_bias,
    cotangent,
):
    gathered = (
        lax.all_gather(w_query, "shard", axis=0, tiled=True),
        lax.all_gather(w_key, "shard", axis=0, tiled=True),
        lax.all_gather(w_value, "shard", axis=0, tiled=True),
        lax.all_gather(w_output, "shard", axis=0, tiled=True),
        lax.all_gather(w_gate, "shard", axis=0, tiled=True),
        lax.all_gather(w_up, "shard", axis=0, tiled=True),
        lax.all_gather(w_down, "shard", axis=0, tiled=True),
        lax.all_gather(norm_attn, "shard", axis=0, tiled=True),
        lax.all_gather(norm_ffn, "shard", axis=0, tiled=True),
        lax.all_gather(rel_bias, "shard", axis=0, tiled=True),
    )
    tokens_f = tokens.astype(jnp.float32)
    length = tokens_f.shape[0]
    output, kept_acts = forward(gathered, tokens_f, segment_ids, buckets)
    back_weights = (
        lax.all_gather(w_query, "shard", axis=0, tiled=True),
        lax.all_gather(w_key, "shard", axis=0, tiled=True),
        lax.all_gather(w_value, "shard", axis=0, tiled=True),
        lax.all_gather(w_output, "shard", axis=0, tiled=True),
        lax.all_gather(w_gate, "shard", axis=0, tiled=True),
        lax.all_gather(w_up, "shard", axis=0, tiled=True),
        lax.all_gather(w_down, "shard", axis=0, tiled=True),
        lax.all_gather(norm_attn, "shard", axis=0, tiled=True),
        lax.all_gather(norm_ffn, "shard", axis=0, tiled=True),
        lax.all_gather(rel_bias, "shard", axis=0, tiled=True),
    )
    unused_out, kept_acts = forward(back_weights, tokens_f, segment_ids, buckets)
    (
        query_full,
        key_full,
        value_full,
        output_full,
        gate_full,
        up_full,
        down_full,
        attn_gain,
        ffn_gain,
        bias_full,
    ) = back_weights
    (
        normed_one,
        inverse_one,
        queries,
        key_rows,
        value_rows,
        table_low,
        attended,
        log_total,
        middle,
        normed_two,
        inverse_two,
        gate_pre,
        up_part,
        hidden,
    ) = kept_acts
    grad_out = cotangent.astype(jnp.float32)
    grad_w_down = product_tn(hidden, cotangent)
    grad_hidden = product_nt(cotangent, down_full)
    activated, gelu_pull = jax.vjp(gelu_tanh, gate_pre)
    grad_gate = gelu_pull(grad_hidden * up_part)[0].astype(jnp.bfloat16)
    grad_up = (grad_hidden * activated).astype(jnp.bfloat16)
    grad_w_gate = product_tn(normed_two, grad_gate)
    grad_w_up = product_tn(normed_two, grad_up)
    grad_normed_two = product_nt(grad_gate, gate_full) + product_nt(grad_up, up_full)
    grad_middle_part, grad_norm_ffn = normalize_back(
        grad_normed_two, middle, inverse_two, ffn_gain.astype(jnp.float32)
    )
    grad_middle = grad_out + grad_middle_part
    grad_branch = grad_middle.astype(jnp.bfloat16)
    grad_w_output = product_tn(attended, grad_branch)
    grad_attended = (
        product_nt(grad_branch, output_full).astype(jnp.bfloat16).reshape(length, HEADS, HD)
    )
    query_blocks, segment_blocks, block_starts = block_inputs(queries, segment_ids)
    grad_att_blocks = grad_attended.reshape(query_blocks.shape)

    def attend_back(carry_acc, inputs):
        grad_keys, grad_values, grad_offsets = carry_acc
        query_block, segment_block, block_start, grad_block, log_block = inputs
        scores = block_scores(
            query_block, segment_block, block_start, key_rows, segment_ids, table_low
        )
        prob_rows = jnp.exp(scores - log_block)
        grad_probs = jnp.einsum(
            "qhd,khd->hqk", grad_block, value_rows, preferred_element_type=jnp.float32
        )
        grad_scores = prob_rows * (
            grad_probs - jnp.sum(prob_rows * grad_probs, axis=-1, keepdims=True)
        )
        grad_low = grad_scores.astype(jnp.bfloat16)
        grad_query = jnp.einsum(
            "hqk,khd->qhd", grad_low, key_rows, preferred_element_type=jnp.float32
        ) * HD ** (-0.5)
        grad_keys = grad_keys + jnp.einsum(
            "hqk,qhd->khd", grad_low, query_block, preferred_element_type=jnp.float32
        ) * HD ** (-0.5)
        grad_values = grad_values + jnp.einsum(
            "hqk,qhd->khd",
            prob_rows.astype(jnp.bfloat16),
            grad_block,
            preferred_element_type=jnp.float32,
        )
        diagonal = diagonal_sums(grad_low, block_start, length)
        return ((grad_keys, grad_values, grad_offsets + diagonal), grad_query)

    zero_rows = jnp.zeros((length, HEADS, HD), jnp.float32)
    zero_offsets = jnp.zeros((HEADS, 2 * length - 1), jnp.float32)
    (grad_keys, grad_values, grad_offsets), grad_q_blocks = lax.scan(
        attend_back,
        (zero_rows, zero_rows, zero_offsets),
        (query_blocks, segment_blocks, block_starts, grad_att_blocks, log_total),
    )
    grad_queries = grad_q_blocks.reshape(length, D).astype(jnp.bfloat16)
    grad_key_rows = grad_keys.reshape(length, D).astype(jnp.bfloat16)
    grad_value_rows = grad_values.reshape(length, D).astype(jnp.bfloat16)
    grad_w_query = product_tn(normed_one, grad_queries)
    grad_w_key = product_tn(normed_one, grad_key_rows)
    grad_w_value = product_tn(normed_one, grad_value_rows)
    grad_normed_one = (
        product_nt(grad_queries, query_full)
        + product_nt(grad_key_rows, key_full)
        + product_nt(grad_value_rows, value_full)
    )
    grad_tokens_part, grad_norm_attn = normalize_back(
        grad_normed_one, tokens_f, inverse_one, attn_gain.astype(jnp.float32)
    )
    grad_tokens = (grad_middle + grad_tokens_part).astype(jnp.bfloat16)
    bucket_onehot = (buckets[:, None] == jnp.arange(NB, dtype=jnp.int32)[None, :]).astype(
        jnp.float32
    )
    grad_rel_bias = jnp.dot(
        bucket_onehot.T, grad_offsets.T, precision=HIGHEST, preferred_element_type=jnp.float32
    )
    (
        share_query,
        share_key,
        share_value,
        share_output,
        share_gate,
        share_up,
        share_down,
        share_attn,
        share_ffn,
        share_bias,
    ) = (
        lax.psum_scatter(
            grad_w_query.astype(jnp.bfloat16), "shard", scatter_dimension=0, tiled=True
        ).astype(jnp.float32),
        lax.psum_scatter(
            grad_w_key.astype(jnp.bfloat16), "shard", scatter_dimension=0, tiled=True
        ).astype(jnp.float32),
        lax.psum_scatter(
            grad_w_value.astype(jnp.bfloat16), "shard", scatter_dimension=0, tiled=True
        ).astype(jnp.float32),
        lax.psum_scatter(
            grad_w_output.astype(jnp.bfloat16), "shard", scatter_dimension=0, tiled=True
        ).astype(jnp.float32),
        lax.psum_scatter(
            grad_w_gate.astype(jnp.bfloat16), "shard", scatter_dimension=0, tiled=True
        ).astype(jnp.float32),
        lax.psum_scatter(
            grad_w_up.astype(jnp.bfloat16), "shard", scatter_dimension=0, tiled=True
        ).astype(jnp.float32),
        lax.psum_scatter(
            grad_w_down.astype(jnp.bfloat16), "shard", scatter_dimension=0, tiled=True
        ).astype(jnp.float32),
        lax.psum_scatter(
            grad_norm_attn.astype(jnp.bfloat16), "shard", scatter_dimension=0, tiled=True
        ).astype(jnp.float32),
        lax.psum_scatter(
            grad_norm_ffn.astype(jnp.bfloat16), "shard", scatter_dimension=0, tiled=True
        ).astype(jnp.float32),
        lax.psum_scatter(
            grad_rel_bias.astype(jnp.bfloat16), "shard", scatter_dimension=0, tiled=True
        ).astype(jnp.float32),
    )
    totals = (
        lax.psum(share_query.astype(jnp.bfloat16), "rep").astype(jnp.float32),
        lax.psum(share_key.astype(jnp.bfloat16), "rep").astype(jnp.float32),
        lax.psum(share_value.astype(jnp.bfloat16), "rep").astype(jnp.float32),
        lax.psum(share_output.astype(jnp.bfloat16), "rep").astype(jnp.float32),
        lax.psum(share_gate.astype(jnp.bfloat16), "rep").astype(jnp.float32),
        lax.psum(share_up.astype(jnp.bfloat16), "rep").astype(jnp.float32),
        lax.psum(share_down.astype(jnp.bfloat16), "rep").astype(jnp.float32),
        lax.psum(share_attn.astype(jnp.bfloat16), "rep").astype(jnp.float32),
        lax.psum(share_ffn.astype(jnp.bfloat16), "rep").astype(jnp.float32),
        lax.psum(share_bias.astype(jnp.bfloat16), "rep").astype(jnp.float32),
    )
    return (
        output.astype(jnp.bfloat16),
        grad_tokens,
        totals[0],
        totals[1],
        totals[2],
        totals[3],
        totals[4],
        totals[5],
        totals[6],
        totals[7],
        totals[8],
        totals[9],
    )


def solution(mesh):
    if tuple(mesh.shape.values()) == (2 * XN, ZN * YN):
        names = ("x", "c", "z", "y")
        mesh = jax.sharding.Mesh(mesh.devices.reshape(XN, 2, ZN, YN), names)
        rep, shard, body = ("x", "c"), ("z", "y"), fast
    else:
        rep, shard, body = ("rep",), ("shard",), shards
    rows = P(rep + shard, None)
    weights = [P(shard, None)] * 7
    gains_spec = [P(shard), P(shard), P(shard, None)]
    return jax.shard_map(
        body,
        mesh=mesh,
        in_specs=(rows, P(rep + shard), P(), *weights, *gains_spec, rows),
        out_specs=(rows, rows, *weights, *gains_spec),
        check_vma=False,
    )
```
